256 devices in a mesh: row: 32 (over y, z), col: 8 (over x, core).
Axes of the slice: x: 4, y: 4, z: 8, core: 2. Of those that a mesh axis runs over, the one named last changes fastest.
Arguments:
- diag_block: float32 [256, 256], P(('row', 'col')), may hold values from -1 to 40, as said below
- panel: float32 [24576, 256], P(('row', 'col')), may hold values from -6 to 6
- trailing: bfloat16 [24576, 24576], P('row', 'col'), may hold values from -6 to 6
Outputs:
- diag_factor: float32 [256, 256], P(('row', 'col'))
- panel_factor: float32 [24576, 256], P(('row', 'col'))
- trailing_out: bfloat16 [24576, 24576], P('row', 'col')
The draws below stay inside these ranges and needn't reach their ends.
Inputs may be any that keep to these rules, and one draw needn't show every extreme that they name: diag_block is symmetric, with off-diagonal entries in -1 to 1 and diagonal entries in 24 to 40, so it is positive definite.
All inputs are finite; a program needn't handle non-finite values.
Results may differ from the reference program's by a relative error of at most 0.001.
Values sent between devices are 32-bit elements; how exact they have to be, the bound alone decides.
No kernel may reach another device: no remote copies, remote signals or barrier semaphores. Data moves between devices by JAX's collectives and lax.ppermute only.
A program may use at most 128 MiB of HBM per device.

```python
import jax
import jax.numpy as jnp
from jax import lax

ORDER = 24576
PANEL = 256
BLOCK = 256
N_ROW = 32
N_COL = 8


def draw_diag_block(key, part):
    first_key, second_key = jax.random.split(key)
    entries = jax.random.uniform(first_key, (PANEL, PANEL), jnp.float32, -1.0, 1.0)
    balanced = 0.5 * (entries + entries.T)
    diag_values = jax.random.uniform(second_key, (PANEL,), jnp.float32, 24.0, 40.0)
    unit_diag = jnp.eye(PANEL, dtype=jnp.float32)
    return balanced * (1.0 - unit_diag) + unit_diag * diag_values[None, :]


def shard_levels(own_key, extent, cuts, low, largest):
    level = 1.0
    for dim, shards_of in cuts:
        draws = jax.random.uniform(jax.random.fold_in(jax.random.fold_in(own_key, 6), dim), (shards_of,), jnp.float32, low / len(cuts), largest / len(cuts))
        level = level * jnp.repeat(jnp.exp(draws), extent[dim] // shards_of).reshape((-1,) + (1,) * (len(extent) - 1 - dim))
    return level


def noise(own_key, extent, deviation, limit, pieces=(), kind=jnp.bfloat16):
    gain = shard_levels(own_key, extent, pieces, -0.22, 0.18) if pieces else 1.0
    result = jax.random.normal(own_key, extent, jnp.float32) * deviation * gain
    return jnp.minimum(jnp.maximum(result, -limit), limit).astype(kind)


def setup_inputs(seed: int = 0) -> dict:
    splits = jax.random.split(jax.random.key(seed), 4)
    return {
        "diag_block": draw_diag_block(jax.random.fold_in(splits[3], 71), 0),
        "panel": noise(splits[1], (ORDER, PANEL), 1.0, 6.0, ((0, 256),), jnp.float32),
        "trailing": noise(splits[2], (ORDER, ORDER), 1.0, 6.0, ((0, 32), (1, 8))),
    }


def reference(diag_block, panel, trailing):
    diag_factor = jnp.linalg.cholesky(diag_block)
    identity = jnp.eye(PANEL, dtype=jnp.float32)
    inverse = lax.linalg.triangular_solve(diag_factor, identity, left_side=True, lower=True)
    panel_factor = jnp.dot(panel.astype(jnp.float32), inverse.T.astype(jnp.float32), precision=lax.Precision.HIGHEST, preferred_element_type=jnp.float32)
    column_ratio = N_ROW // N_COL
    per_block = ORDER // N_ROW // BLOCK
    grouped = panel_factor.reshape(column_ratio, N_COL, per_block, BLOCK, PANEL)
    column_panel = jnp.transpose(grouped, (1, 2, 0, 3, 4)).reshape(ORDER, PANEL)
    row_step = min(ORDER, 512)
    stacked_rows = panel_factor.reshape(ORDER // row_step, row_step, PANEL)
    stacked_trailing = trailing.reshape(ORDER // row_step, row_step, ORDER)

    def one_block(operands):
        factor_rows, trailing_rows = operands
        update = jnp.dot(factor_rows.astype(jnp.float32), column_panel.T.astype(jnp.float32), precision=lax.Precision.HIGHEST, preferred_element_type=jnp.float32)
        return (trailing_rows.astype(jnp.float32) - update).astype(jnp.bfloat16)
    trailing_out = lax.map(one_block, (stacked_rows, stacked_trailing)).reshape(ORDER, ORDER)
    return (diag_factor, panel_factor, trailing_out)
```

```python
import jax
import jax.numpy as jnp
from jax import lax
from jax.sharding import PartitionSpec as P

BLOCK = 256
GRID = ("row", "col")
HIGHEST = lax.Precision.HIGHEST
HIGH = lax.Precision.HIGH


def product(a, b, precision=HIGHEST):
    return jnp.dot(a, b, precision=precision, preferred_element_type=jnp.float32)


def per_device(diag_block, panel, trailing):
    count_rows, count_cols = lax.axis_size("row"), lax.axis_size("col")
    devices = count_rows * count_cols
    ratio = count_rows // count_cols
    panel_width = panel.shape[1]

    swap = [
        ((r * count_cols + a) * count_cols + b, (r * count_cols + b) * count_cols + a)
        for r in range(ratio)
        for a in range(count_cols)
        for b in range(count_cols)
    ]
    moved = lax.ppermute(panel, GRID, swap)
    column_rows = lax.all_gather(moved, "row", axis=0, tiled=True)

    diag_share = diag_block.shape[0]
    copies = jnp.broadcast_to(diag_block[None], (devices,) + diag_block.shape)
    copies = copies.reshape(devices * diag_share, panel_width)
    whole_diag = lax.all_to_all(copies, GRID, 0, 0, tiled=True)
    row_rows = lax.all_gather(panel, "col", axis=0, tiled=True)

    diag_factor = jnp.linalg.cholesky(whole_diag)
    identity = jnp.eye(panel_width, dtype=jnp.float32)
    inverse = lax.linalg.triangular_solve(diag_factor, identity, left_side=True, lower=True)
    panel_factor = product(panel, inverse.T)
    factor_rows = lax.dynamic_slice_in_dim(
        diag_factor, lax.axis_index(GRID) * diag_share, diag_share, 0
    )
    left = product(product(row_rows, inverse.T), inverse)
    per_block = row_rows.shape[0] // BLOCK
    grouped = column_rows.reshape(ratio, per_block, BLOCK, panel_width)
    right = jnp.transpose(grouped, (1, 0, 2, 3)).reshape(-1, panel_width)
    update = product(left, right.T, HIGH)
    trailing_out = (trailing.astype(jnp.float32) - update).astype(jnp.bfloat16)
    return (factor_rows, panel_factor, trailing_out)


def solution(mesh):
    placed = (P(GRID, None), P(GRID, None), P("row", "col"))
    return jax.shard_map(
        per_device,
        mesh=mesh,
        in_specs=placed,
        out_specs=placed,
        check_vma=False,
    )
```

```python
import functools

import jax
import jax.numpy as jnp
from jax import lax
from jax.experimental import pallas as pl
from jax.experimental.pallas import tpu as pltpu
from jax.sharding import PartitionSpec as P


GRID = ("row", "col")
LANES = 128
SUB = 8
BLOCK = 256
F32 = jnp.float32
BF16 = jnp.bfloat16


def dot(a, b, dims=((1,), (0,))):
    return lax.dot_general(
        a, b, (dims, ((), ())), precision=lax.Precision.HIGHEST, preferred_element_type=F32
    )


def pair_inverse(d1, d12, d2):
    r = 1.0 / (d1 * d2 - d12 * d12)
    return d2 * r, -(d12 * r), d1 * r


def factor_half(block):
    groups = LANES // SUB
    full = (SUB, LANES)
    a = [block[SUB * g : SUB * (g + 1), :] for g in range(groups)]
    lane = lax.broadcasted_iota(jnp.int32, full, 1)
    sub = lax.broadcasted_iota(jnp.int32, full, 0)
    w = [jnp.where(lane == sub + SUB * g, 1.0, 0.0).astype(F32) for g in range(groups)]

    def col(v, k):
        return jnp.broadcast_to(v[:, k : k + 1], full)

    def row(v, s):
        return jnp.broadcast_to(v[s : s + 1, :], full)

    def pack(r):
        o = r[0]
        for s in range(1, SUB):
            o = jnp.where(sub == s, r[s], o)
        return o

    done_a, done_w = [], []
    for g in range(groups):
        k = SUB * g
        ra = [row(a[g], s) for s in range(SUB)]
        rw = [row(w[g], s) for s in range(SUB)]
        cols = [col(a[g], k + j) for j in range(SUB)]
        e = {(i, j): row(cols[j], i) for i in range(SUB) for j in range(i, SUB)}
        xa, xw, t = [None] * SUB, [None] * SUB, {}
        for p in range(0, SUB, 2):
            q = p + 1
            i1, i12, i2 = pair_inverse(e[p, p], e[p, q], e[q, q])
            for j in range(p + 2, SUB):
                t[p, j] = i1 * e[p, j] + i12 * e[q, j]
                t[q, j] = i12 * e[p, j] + i2 * e[q, j]
            for j in range(p + 2, SUB):
                for m in range(j, SUB):
                    e[j, m] = e[j, m] - (t[p, j] * e[p, m] + t[q, j] * e[q, m])
            for x, r in ((xa, ra), (xw, rw)):
                x[p] = i1 * r[p] + i12 * r[q]
                x[q] = i12 * r[p] + i2 * r[q]
                for j in range(p + 2, SUB):
                    r[j] = r[j] - (t[p, j] * r[p] + t[q, j] * r[q])
        for i in range(SUB - 4, -1, -2):
            for x in (xa, xw):
                for p in (i, i + 1):
                    for j in range(i + 2, SUB, 2):
                        x[p] = x[p] - (t[p, j] * x[j] + t[p, j + 1] * x[j + 1])
        for i in range(g + 1, groups):
            c = [col(a[i], k + j) for j in range(SUB)]
            for y, x in ((a, xa), (w, xw)):
                s = [c[j] * x[j] + c[j + 1] * x[j + 1] for j in range(0, SUB, 2)]
                y[i] = y[i] - ((s[0] + s[1]) + (s[2] + s[3]))
        done_a.append(pack(ra))
        done_w.append(pack(rw))
    a, w = jnp.concatenate(done_a, 0), jnp.concatenate(done_w, 0)

    rows = lax.broadcasted_iota(jnp.int32, (LANES, LANES), 0)
    lanes = lax.broadcasted_iota(jnp.int32, (LANES, LANES), 1)
    odd = rows[:, :1] % 2 == 1
    before_a = pltpu.roll(a, 1, 0)
    before_w = pltpu.roll(w, 1, 0)

    def pick(v, where):
        return jnp.sum(jnp.where(where, v, 0.0), axis=1, keepdims=True)

    diag = pick(a, lanes == rows)
    d12 = jnp.where(odd, pick(before_a, lanes == rows), 0.0)
    d1 = jnp.where(odd, pick(before_a, lanes == rows - 1), 1.0)
    q = d12 / d1
    scale = lax.rsqrt(diag - q * d12)
    u = jnp.where(lanes >= rows, (a - q * before_a) * scale, 0.0)
    w = jnp.where(lanes <= rows, (w - q * before_w) * scale, 0.0)
    return u, w


def pack_kernel(at, diag, panel, out):
    rows = panel.shape[0]
    out[:rows, :] = panel[...]
    spot = lax.broadcasted_iota(jnp.int32, (SUB, panel.shape[1]), 0) == at[2] * 2 + at[3]
    out[rows:, :] = jnp.where(spot, diag[...], 0.0)


def total_kernel(p0, p1, p2, p3, others, out):
    size = p0.shape[0]
    total = (p0[size - SUB :, :] + p1[size - SUB :, :]) + (p2[size - SUB :, :] + p3[size - SUB :, :])
    for n in range(4):
        total = total + others[size * (n + 1) - SUB : size * (n + 1), :]
    out[...] = total


def load_kernel(panel, d0, d1, d2, d3, out):
    rows = panel.shape[0]
    out[:rows, :] = panel[...]
    for n, d in enumerate((d0, d1, d2, d3)):
        out[rows + SUB * n : rows + SUB * (n + 1), :] = d[...]


TURNS = (0, 3, 1, 2)
AROUND = (-1, 0, 1, -2, 2, -3, 3, -4)


def factor_kernel(at, *refs):
    ring, parts, others = refs[:8], refs[8:12], refs[12]
    panel, row_out, f_out, g_out, a, lower, w, left = refs[13:]
    y, z, x, core, flat = at[0], at[1], at[2], at[3], at[4]
    rows = panel.shape[0]
    for load, off in zip(ring, AROUND):
        for m, dy in enumerate(TURNS):
            to = (lax.rem(y + dy, 4) * 8 + lax.rem(z + off + 8, 8)) * SUB
            a[pl.ds(pl.multiple_of(to, SUB), SUB), :] = load[rows + SUB * m : rows + SUB * (m + 1), :]
    h = LANES
    u11, w11 = factor_half(a[:h, :h])
    l21 = dot(a[h:, :h], w11, ((1,), (1,)))
    u22, w22 = factor_half(a[h:, h:] - dot(l21, l21, ((1,), (1,))))
    w21 = -dot(w22, dot(l21, w11))
    zero = jnp.zeros((h, h), F32)
    lower[:h, :h] = u11.T
    lower[:h, h:] = zero
    lower[h:, :h] = l21
    lower[h:, h:] = u22.T
    row_out[...] = lower[pl.ds(flat, 1), :]
    w[:h, :h] = w11
    w[:h, h:] = zero
    w[h:, :h] = w21
    w[h:, h:] = w22
    f_out[...] = dot(panel[...], w[...], ((1,), (1,)))
    inverse = dot(w[...], w[...], ((0,), (0,)))
    size = rows + SUB
    for n, dx in enumerate((0, 3, 1, 2)):
        for c, part in ((core, parts[n][:rows, :]), (1 - core, others[size * n : size * n + rows, :])):
            to = pl.multiple_of((lax.rem(x + dx, 4) * 2 + c) * rows, rows)
            left[pl.ds(to, rows), :] = part
    g = dot(left[...], inverse)
    high = g.astype(BF16)
    g_out[:, :BLOCK] = high
    g_out[:, BLOCK : 2 * BLOCK] = high
    g_out[:, 2 * BLOCK :] = (g - high.astype(F32)).astype(BF16)


def update_kernel(dy, places, at, g, trailing, *refs):
    out, wide = refs[-2:]
    step = pl.program_id(0)
    rows = g.shape[0] // 8

    @pl.when(step == 0)
    def _():
        for (ref, start), off in zip(places, AROUND):
            to = pl.ds(pl.multiple_of(lax.rem(at[1] + off + 8, 8) * rows, rows), rows)
            value = refs[ref][start : start + rows, :]
            high = value.astype(BF16)
            wide[to, :BLOCK] = high
            wide[to, BLOCK : 2 * BLOCK] = (value - high.astype(F32)).astype(BF16)
            wide[to, 2 * BLOCK :] = high

    column = pl.multiple_of((step * 4 + lax.rem(at[0] + dy, 4)) * BLOCK, BLOCK)
    here = wide[pl.ds(pl.multiple_of(step * BLOCK, BLOCK), BLOCK), :]
    update = lax.dot_general(g[...], here, (((1,), (1,)), ((), ())), preferred_element_type=F32)
    out[...] = (trailing[:, pl.ds(column, BLOCK)].astype(F32) - update).astype(BF16)


def kernel_call(body, out_shape, scalars, *args, scratch=(), flops=0, limit=4):
    whole = pl.BlockSpec(memory_space=pltpu.VMEM)
    many = isinstance(out_shape, list)
    return pl.pallas_call(
        body,
        out_shape=out_shape,
        grid_spec=pltpu.PrefetchScalarGridSpec(
            num_scalar_prefetch=len(scalars),
            grid=(),
            in_specs=[whole] * len(args),
            out_specs=[whole] * len(out_shape) if many else whole,
            scratch_shapes=list(scratch),
        ),
        compiler_params=pltpu.CompilerParams(vmem_limit_bytes=limit << 20),
        cost_estimate=pl.CostEstimate(flops=flops, bytes_accessed=10**5, transcendentals=0),
    )(*scalars, *args)


def update(at, g, pieces, places, trailing, before, dy):
    tile = (trailing.shape[0], BLOCK)

    def place(i, at):
        return (0, i * 4 + lax.rem(at[0] + dy, 4))

    whole = pl.BlockSpec(memory_space=pltpu.VMEM)
    in_specs = [whole] * (2 + len(pieces))
    args = [g, trailing, *pieces]
    alias = {}
    if before is not None:
        in_specs.append(pl.BlockSpec(memory_space=pl.ANY))
        args.append(before)
        alias = {len(args): 0}
    return pl.pallas_call(
        functools.partial(update_kernel, dy, places),
        out_shape=jax.ShapeDtypeStruct(trailing.shape, BF16),
        grid_spec=pltpu.PrefetchScalarGridSpec(
            num_scalar_prefetch=1,
            grid=(3,),
            in_specs=in_specs,
            out_specs=pl.BlockSpec(tile, place),
            scratch_shapes=[pltpu.VMEM((3 * BLOCK, 3 * BLOCK), BF16)],
        ),
        input_output_aliases=alias,
        compiler_params=pltpu.CompilerParams(vmem_limit_bytes=12 << 20),
        cost_estimate=pl.CostEstimate(flops=2 * 768**3, bytes_accessed=4 * 768**2, transcendentals=0),
    )(at, *args)


def move(value, function):
    pairs = []
    for y in range(4):
        for z in range(8):
            for x in range(4):
                for c in range(2):
                    ty, tz, tx, tc = function(y, z, x, c)
                    source = ((y * 8 + z) * 4 + x) * 2 + c
                    target = (((ty % 4) * 8 + tz % 8) * 4 + tx % 4) * 2 + tc % 2
                    pairs.append((source, target))
    return lax.ppermute(value, GRID, pairs)


def along_y(value, s):
    return move(value, lambda y, z, x, c: (y + s, z, x, c))


def along_x(value, s):
    return move(value, lambda y, z, x, c: (y, z, x + s, c))


def along_z(value, s):
    return move(value, lambda y, z, x, c: (y, z + s, x, c))


def per_device(diag_block, panel, trailing):
    row, col = lax.axis_index("row"), lax.axis_index("col")
    at = jnp.stack([row // 8, row % 8, col // 2, col % 2, row * 8 + col]).astype(jnp.int32)
    rows, width = panel.shape

    def shape(*dims, kind=F32):
        return jax.ShapeDtypeStruct(dims, kind)

    moved = move(panel, lambda y, z, x, c: (y, 2 * x + c, z // 2, z % 2))

    load = kernel_call(pack_kernel, shape(rows + SUB, width), [at], diag_block, panel)
    mine = [load] + [along_x(load, s) for s in (1, -1, 2)]
    other = move(jnp.concatenate(mine, 0), lambda y, z, x, c: (y, z, x, 1 - c))
    diag8 = kernel_call(total_kernel, shape(SUB, width), [], *mine, other)
    ds = [along_y(diag8, s) for s in (1, -1, 2)]

    load = kernel_call(load_kernel, shape(rows + 4 * SUB, width), [], moved, diag8, *ds)
    up, down = [load], [load]
    for n in range(1, 5):
        up.append(along_z(up[-1], 1))
        if n < 4:
            down.append(along_z(down[-1], -1))
    ring = [up[1], load, down[1], up[2], down[2], up[3], down[3], up[4]]
    blocks = [v[:rows] for v in ring]
    first, last = jnp.concatenate(blocks[:3], 0), jnp.concatenate(blocks[3:], 0)
    fa = [along_y(first, s) for s in (1, -1)]
    fb = [along_y(last, s) for s in (1, -1)]
    far = [along_y(jnp.concatenate([first, last[:rows]], 0), 2), along_y(last[rows:], -2)]

    factor_row, factor_rows, left = kernel_call(
        factor_kernel,
        [shape(1, width), shape(rows, width), shape(8 * rows, 3 * width, kind=BF16)],
        [at], *ring, *mine, other, panel,
        scratch=[pltpu.VMEM((width, width), F32)] * 3 + [pltpu.VMEM((8 * rows, width), F32)],
        flops=10**10, limit=12,
    )
    near = [(0, n * rows) for n in range(3)] + [(1, n * rows) for n in range(5)]
    away = [(0, n * rows) for n in range(4)] + [(1, n * rows) for n in range(4)]
    out = update(at, left, ring, [(n, 0) for n in range(8)], trailing, None, 0)
    out = update(at, left, [fa[0], fb[0]], near, trailing, out, 3)
    out = update(at, left, [fa[1], fb[1]], near, trailing, out, 1)
    out = update(at, left, far, away, trailing, out, 2)
    return (factor_row, factor_rows, out)


def solution(mesh):
    placed = (P(GRID, None), P(GRID, None), P("row", "col"))
    return jax.shard_map(per_device, mesh=mesh, in_specs=placed, out_specs=placed, check_vma=False)
```
